32 devices in a mesh: party: 2 (over x), sample: 8 (over z, core), feat: 2 (over y).
Axes of the slice: x: 2, y: 2, z: 4, core: 2. Of those that a mesh axis runs over, the one named last changes fastest.
Arguments:
- x_share: bfloat16 [2, 2048, 8192], P('party', 'sample', 'feat'), may hold values from -3 to 3
- a_share: bfloat16 [2, 2048, 8192], P('party', 'sample', 'feat'), may hold values from -3 to 3
- w_share: float32 [2, 8192, 256], P('party', 'feat'), may hold values from -0.0625 to 0.0625
- b_share: bfloat16 [2, 8192, 256], P('party', 'feat'), may hold values from -0.0625 to 0.0625
- c_share: bfloat16 [2, 2048, 256], P('party', 'sample'), may hold values from -6 to 6
- mask_lin: bfloat16 [2, 2048, 256], P('party', 'sample'), may hold values from -12 to 12
- mask_sq: bfloat16 [2, 2048, 256], P('party', 'sample'), may hold values from -30 to 30
- mask_cube: bfloat16 [2, 2048, 256], P('party', 'sample'), may hold values from -240 to 240
- y_share: bfloat16 [2, 2048, 256], P('party', 'sample'), may hold values from -6 to 6
- r_mask: bfloat16 [2, 2048, 256], P('party', 'sample'), may hold values from -3 to 3
- grad_product: bfloat16 [2, 8192, 256], P('party', 'feat'), may hold values from -240 to 240
Outputs:
- new_weights: float32 [2, 8192, 256], P('party', 'feat')
The draws below stay inside these ranges and needn't reach their ends.
All inputs are finite; a program needn't handle non-finite values.
Results may differ from the reference program's by a relative error of at most 0.0018.
Values may be sent and summed in bfloat16 or wider, within the bound.
No kernel may reach another device: no remote copies, remote signals or barrier semaphores. Data moves between devices by JAX's collectives and lax.ppermute only.
A program may use at most 64 MiB of HBM per device.

```python
import jax
import jax.numpy as jnp

FEATURES = 8192
PHENO = 256
SAMPLES = 2048


def steps_of(key, extent, split, least, high):
    def one(dim, parts):
        draws = jax.random.uniform(jax.random.fold_in(jax.random.fold_in(key, 6), dim), (parts,), jnp.float32, least / len(split), high / len(split))
        return jnp.repeat(jnp.exp(draws), extent[dim] // parts).reshape((-1,) + (1,) * (len(extent) - dim - 1))

    gain = one(*split[0])
    for cut in split[1:]:
        gain = gain * one(*cut)
    return gain


def noise(own_key, extent, scale, reach, pieces=(), dtype=jnp.bfloat16):
    result = jax.random.normal(own_key, extent, jnp.float32) * scale
    if len(pieces) > 0:
        result = steps_of(own_key, extent, pieces, -0.22, 0.18) * result
    return jnp.clip(result, min=-reach, max=reach).astype(dtype)


def setup_inputs(seed: int = 0) -> dict:
    arg_keys = jax.random.split(jax.random.key(seed), 12)
    return {
        "x_share": noise(arg_keys[0], (2, SAMPLES, FEATURES), 0.5, 3.0, ((0, 2), (1, 8), (2, 2))),
        "a_share": noise(arg_keys[1], (2, SAMPLES, FEATURES), 0.5, 3.0, ((0, 2), (1, 8), (2, 2))),
        "w_share": noise(arg_keys[2], (2, FEATURES, PHENO), FEATURES ** -0.5, 0.0625, ((0, 2), (1, 2)), jnp.float32),
        "b_share": noise(arg_keys[3], (2, FEATURES, PHENO), FEATURES ** -0.5, 0.0625, ((0, 2), (1, 2))),
        "c_share": noise(arg_keys[4], (2, SAMPLES, PHENO), 1.0, 6.0, ((0, 2), (1, 8))),
        "mask_lin": noise(arg_keys[5], (2, SAMPLES, PHENO), 2.0, 12.0, ((0, 2), (1, 8))),
        "mask_sq": noise(arg_keys[6], (2, SAMPLES, PHENO), 5.0, 30.0, ((0, 2), (1, 8))),
        "mask_cube": noise(arg_keys[7], (2, SAMPLES, PHENO), 40.0, 240.0, ((0, 2), (1, 8))),
        "y_share": noise(arg_keys[8], (2, SAMPLES, PHENO), 1.0, 6.0, ((0, 2), (1, 8))),
        "r_mask": noise(arg_keys[9], (2, SAMPLES, PHENO), 0.5, 3.0, ((0, 2), (1, 8))),
        "grad_product": noise(arg_keys[10], (2, FEATURES, PHENO), 40.0, 240.0, ((0, 2), (1, 2))),
    }


learn_rate = 64.0
slope_one = 0.197
cube_coef = 0.004


def reference(x_share, a_share, w_share, b_share, c_share, mask_lin, mask_sq, mask_cube, y_share, r_mask, grad_product):
    masked_inputs = (x_share.astype(jnp.float32) - a_share.astype(jnp.float32)).astype(jnp.bfloat16)
    opened_inputs = (masked_inputs[0].astype(jnp.float32) + masked_inputs[1].astype(jnp.float32)).astype(jnp.bfloat16)
    masked_weights = (w_share - b_share.astype(jnp.float32)).astype(jnp.bfloat16)
    opened_weights = (masked_weights[0].astype(jnp.float32) + masked_weights[1].astype(jnp.float32)).astype(jnp.bfloat16)
    both_terms = jnp.dot(opened_inputs, opened_weights, preferred_element_type=jnp.float32)
    margins = []
    for party in range(2):
        select = 1.0 if party == 0 else 0.0
        margin = select * both_terms
        margin = margin + jnp.dot(opened_inputs, b_share[party], preferred_element_type=jnp.float32)
        margin = margin + jnp.dot(a_share[party], opened_weights, preferred_element_type=jnp.float32)
        margins.append(margin + c_share[party].astype(jnp.float32))
    spread = (margins[0] - mask_lin[0].astype(jnp.float32)) + (margins[1] - mask_lin[1].astype(jnp.float32))
    masked_parts = []
    for party in range(2):
        select = 1.0 if party == 0 else 0.0
        linear = mask_lin[party].astype(jnp.float32)
        cubed = select * (spread * spread * spread) + 3.0 * (spread * spread) * linear
        cubed = cubed + 3.0 * spread * mask_sq[party].astype(jnp.float32) + mask_cube[party].astype(jnp.float32)
        residual = 0.5 * select + slope_one * margins[party] - cube_coef * cubed - y_share[party].astype(jnp.float32)
        masked_parts.append((residual - r_mask[party].astype(jnp.float32)).astype(jnp.bfloat16))
    opened_residual = (masked_parts[0].astype(jnp.float32) + masked_parts[1].astype(jnp.float32)).astype(jnp.bfloat16)
    samples = x_share.shape[1]
    inputs_t = opened_inputs.T
    public_term = jnp.dot(inputs_t, opened_residual, preferred_element_type=jnp.float32)
    results = []
    for party in range(2):
        select = 1.0 if party == 0 else 0.0
        gradient = select * public_term
        gradient = gradient + jnp.dot(inputs_t, r_mask[party], preferred_element_type=jnp.float32)
        gradient = gradient + jnp.dot(a_share[party].T, opened_residual, preferred_element_type=jnp.float32)
        gradient = gradient + grad_product[party].astype(jnp.float32)
        results.append(w_share[party] - (learn_rate / samples) * gradient)
    return jnp.stack(results)
```

```python
import jax
import jax.numpy as jnp
from jax import lax
from jax.sharding import PartitionSpec as P

learn_rate = 64.0
slope_one = 0.197
cube_coef = 0.004
input_reach = 3.0
mask_reach = 3.0
chunks = 4

f32 = jnp.float32
bf16 = jnp.bfloat16
f16 = jnp.float16


def swap(value, axes, size, bit):
    return lax.ppermute(value, axes, [(i, i ^ bit) for i in range(size)])


def narrow(value, dtype):
    info = jnp.finfo(dtype)
    return lax.reduce_precision(value, info.nexp, info.nmant).astype(dtype)


def dot(left, right):
    return jnp.dot(left, right, preferred_element_type=f32)


def dot_rows(left, right):
    return lax.dot_general(left, right, (((0,), (0,)), ((), ())), preferred_element_type=f32)


def rows(array, first, number):
    return lax.dynamic_slice_in_dim(array, first, number, 0)


def shards(x, a, w, b, c_sh, lin, sq, cube, y, r, gp):
    x, a, w, b, gp = x[0], a[0], w[0], b[0], gp[0]
    small = (c_sh[0], lin[0], sq[0], cube[0], y[0], r[0])
    n_sample, n_feat, n_party = (lax.axis_size(k) for k in ("sample", "feat", "party"))
    party, s, feat = (lax.axis_index(k) for k in ("party", "sample", "feat"))
    core = s % 2
    chip = s // 2
    n_chip = n_sample // 2
    group = ("party", "feat")
    n_group = n_party * n_feat
    me = party * n_feat + feat
    samples = x.shape[0]
    half = x.shape[1] // 2
    first = core == 0
    select = (party == 0).astype(f32)

    def core_swap(v):
        return swap(v, "sample", n_sample, 1)

    def party_swap(v):
        return swap(v, "party", n_party, 1)

    def pick(v):
        return jnp.where(first, v[:, :half], v[:, half:]), jnp.where(first, v[:, half:], v[:, :half])

    slab = half // n_chip
    at = core * half + chip * slab
    w_m = narrow(rows(w, at, slab) - rows(b, at, slab).astype(f32), bf16)
    w_o = party_swap(w_m)

    m = narrow(x.astype(f32) - a.astype(f32), bf16)
    m_mine, m_send = pick(m)
    a_mine, a_send = pick(a)
    m_oth = core_swap(m_send)
    o_mine = party_swap(m_mine)
    a_oth = core_swap(a_send)
    o_oth = party_swap(m_oth)

    d_slab = narrow(w_m.astype(f32) + w_o.astype(f32), bf16)
    opened_w = jnp.zeros((half, w.shape[1]), bf16)
    opened_w = lax.dynamic_update_slice_in_dim(opened_w, d_slab, chip * slab, 0)
    for j in range(1, n_chip):
        got = swap(d_slab, "sample", n_sample, 2 * j)
        opened_w = lax.dynamic_update_slice_in_dim(opened_w, got, (chip ^ j) * slab, 0)
    b_half = rows(b, core * half, half)
    d_sel = opened_w * select.astype(bf16)

    r_own = small[5]
    r_oth = core_swap(r_own)
    block = samples // n_group
    theirs = (me ^ n_feat) * block
    packed = jnp.concatenate([rows(v, theirs, block) for v in small], 0)
    packed = party_swap(packed)
    other_small = [packed[k * block : (k + 1) * block].astype(f32) for k in range(6)]
    own_small = [rows(v, me * block, block).astype(f32) for v in small]

    def opened(p, q):
        return narrow(p.astype(f32) + q.astype(f32), bf16)

    e_own = opened(m_mine, o_mine)
    e_oth = opened(m_oth, o_oth)

    def part(e, av):
        return dot(e, d_sel) + dot(e, b_half) + dot(av, opened_w)

    p_own = part(e_own, a_mine)
    p_oth = part(e_oth, a_oth)
    p_sum = p_own + core_swap(p_oth)

    sums = {0: rows(p_sum, me * block, block)}
    for j in range(1, n_group):
        got = swap(rows(p_sum, (me ^ j) * block, block), group, n_group, j)
        q = j // n_feat
        sums[q] = sums[q] + got if q in sums else got

    def shifted(total, arrays):
        margin = total + arrays[0]
        return margin, margin - arrays[1]

    m_a, d_a = shifted(sums[0], own_small)
    m_b, d_b = shifted(sums[1], other_small)
    spread = d_a + d_b

    def masked_residual(margin, arrays, sel):
        _, l, q, k, lab, mask = arrays
        cubed = sel * (spread * spread * spread) + 3.0 * (spread * spread) * l
        cubed = cubed + 3.0 * spread * q + k
        res = 0.5 * sel + slope_one * margin - cube_coef * cubed - lab
        return narrow(res - mask, bf16)

    res = opened(masked_residual(m_a, own_small, select), masked_residual(m_b, other_small, 1.0 - select))

    res_own = jnp.zeros((samples, w.shape[1]), bf16)
    res_own = lax.dynamic_update_slice_in_dim(res_own, res, me * block, 0)
    for j in range(1, n_group):
        got = swap(res, group, n_group, j)
        res_own = lax.dynamic_update_slice_in_dim(res_own, got, (me ^ j) * block, 0)
    res_oth = core_swap(res_own)

    top = jnp.maximum(jnp.max(jnp.abs(res_own)), jnp.max(jnp.abs(res_oth))).astype(f32)
    tops = jnp.full((8, 128), top)
    for j in range(1, n_chip):
        tops = jnp.maximum(tops, swap(jnp.full((8, 128), top), "sample", n_sample, 2 * j))
    top = jnp.max(tops)
    total_samples = samples * n_sample
    bound = total_samples * (5.0 * input_reach * top + 4.0 * input_reach * mask_reach)
    power = jnp.ceil(jnp.log2(bound)) - 15.0
    shrink = jnp.exp2(-power)
    grow = 1.0 / shrink

    rs_own = res_own * select.astype(bf16)
    rs_oth = res_oth * select.astype(bf16)
    early = dot_rows(e_own, r_own) + dot_rows(e_oth, r_oth)
    late = dot_rows(e_own, rs_own) + dot_rows(e_oth, rs_oth)
    late = late + dot_rows(a_mine, res_own) + dot_rows(a_oth, res_oth)
    grad = early + late

    def chip_pairs(pairs):
        return [(2 * i + k, 2 * j + k) for i, j in pairs for k in (0, 1)]

    middle = n_chip // 2
    step = half // chunks
    totals = []
    for k in range(chunks):
        v = grad[k * step : (k + 1) * step] * shrink
        for d in range(middle - 1):
            pairs = chip_pairs([(d, d + 1), (n_chip - 1 - d, n_chip - 2 - d)])
            v = v + lax.ppermute(narrow(v, f16), "sample", pairs).astype(f32)
        u = narrow(v, f16)
        pairs = chip_pairs([(middle - 1, middle), (middle, middle - 1)])
        t = narrow(u.astype(f32) + lax.ppermute(u, "sample", pairs).astype(f32), f16)
        for d in reversed(range(middle - 1)):
            pairs = chip_pairs([(d + 1, d), (n_chip - 2 - d, n_chip - 1 - d)])
            got = lax.ppermute(t, "sample", pairs)
            t = jnp.where((chip == d) | (chip == n_chip - 1 - d), got, t)
        totals.append((t, core_swap(t)))
    mine = jnp.concatenate([t for t, _ in totals], 0)
    theirs = jnp.concatenate([t for _, t in totals], 0)
    low = jnp.where(first, mine, theirs)
    high = jnp.where(first, theirs, mine)
    whole = jnp.concatenate([low, high], 0).astype(f32) * grow + gp.astype(f32)
    return (w - learn_rate / total_samples * whole)[None]


def solution(mesh):
    placed = (
        P("party", "sample", "feat"),
        P("party", "sample", "feat"),
        P("party", "feat", None),
        P("party", "feat", None),
        P("party", "sample", None),
        P("party", "sample", None),
        P("party", "sample", None),
        P("party", "sample", None),
        P("party", "sample", None),
        P("party", "sample", None),
        P("party", "feat", None),
    )
    return jax.shard_map(
        shards, mesh=mesh, in_specs=placed, out_specs=P("party", "feat", None), check_vma=False
    )
```

```python
import jax
import jax.numpy as jnp
from jax import lax
from jax.experimental import pallas as pl
from jax.experimental.pallas import tpu as pltpu
from jax.sharding import PartitionSpec as P


learn_rate = 64.0
slope_one = 0.197
cube_coef = 0.004
input_reach = 3.0
mask_reach = 3.0
chunks = 4

f32 = jnp.float32
bf16 = jnp.bfloat16
f16 = jnp.float16


def swap(value, axes, size, bit):
    return lax.ppermute(value, axes, [(i, i ^ bit) for i in range(size)])


def after(value, token):
    return lax.optimization_barrier((value, token))[0]


def narrow(value, dtype):
    info = jnp.finfo(dtype)
    return lax.reduce_precision(value, info.nexp, info.nmant).astype(dtype)


def opened(p, q):
    return narrow(p.astype(f32) + q.astype(f32), bf16)


def dot(left, right):
    return jnp.dot(left, right, preferred_element_type=f32)


def dot_rows(left, right):
    return lax.dot_general(left, right, (((0,), (0,)), ((), ())), preferred_element_type=f32)


def rows(array, first, number):
    return lax.dynamic_slice_in_dim(array, first, number, 0)


def pack_rows(arrays, block_index, block):
    width = arrays[0].shape[1]

    def body(index, *refs):
        for k, ref in enumerate(refs[:-1]):
            refs[-1][k * block : (k + 1) * block, :] = ref[...]

    spec = pl.BlockSpec((block, width), lambda i, index: (index[0], 0))
    number = len(arrays) * block
    return pl.pallas_call(
        body,
        out_shape=jax.ShapeDtypeStruct((number, width), arrays[0].dtype),
        grid_spec=pltpu.PrefetchScalarGridSpec(
            num_scalar_prefetch=1,
            grid=(1,),
            in_specs=[spec] * len(arrays),
            out_specs=pl.BlockSpec((number, width), lambda i, index: (0, 0)),
        ),
        cost_estimate=pl.CostEstimate(flops=0, bytes_accessed=4 * number * width, transcendentals=0),
        name="pack_rows",
    )(jnp.reshape(block_index, (1,)), *arrays)


def step_fn(x, a, w, b, c_sh, lin, sq, cube, y, r, gp):
    x, a, w, b, gp = x[0], a[0], w[0], b[0], gp[0]
    small = (c_sh[0], lin[0], sq[0], cube[0], y[0], r[0])
    n_sample, n_feat, n_party = (lax.axis_size(k) for k in ("sample", "feat", "party"))
    party, s, feat = (lax.axis_index(k) for k in ("party", "sample", "feat"))
    core = s % 2
    chip = s // 2
    n_chip = n_sample // 2
    group = ("party", "feat")
    n_group = n_party * n_feat
    me = party * n_feat + feat
    samples = x.shape[0]
    pheno = w.shape[1]
    half = x.shape[1] // 2
    quarter = half // 2
    first = core == 0
    select = (party == 0).astype(f32)
    total_samples = samples * n_sample
    rate = learn_rate / total_samples

    def core_swap(v):
        return swap(v, "sample", n_sample, 1)

    def party_swap(v):
        return swap(v, "party", n_party, 1)

    def pick(v):
        return jnp.where(first, v[:, :half], v[:, half:]), jnp.where(first, v[:, half:], v[:, :half])

    slab = half // n_chip
    at = core * half + chip * slab
    w_m = narrow(rows(w, at, slab) - rows(b, at, slab).astype(f32), bf16)
    w_o = party_swap(w_m)

    m = narrow(x.astype(f32) - a.astype(f32), bf16)
    m_mine, m_send = pick(m)
    a_mine, a_send = pick(a)
    m_oth = core_swap(m_send)
    own_a, own_b = m_mine[:, :quarter], m_mine[:, quarter:]
    o_own_a = party_swap(own_a)
    o_oth = party_swap(m_oth)
    o_own_b = party_swap(own_b)
    a_oth = core_swap(a_send)
    r_own = small[5]
    r_oth = core_swap(r_own)

    d_slab = opened(w_m, w_o)
    opened_w = jnp.zeros((half, pheno), bf16)
    opened_w = lax.dynamic_update_slice_in_dim(opened_w, d_slab, chip * slab, 0)
    for j in range(1, n_chip):
        got = swap(d_slab, "sample", n_sample, 2 * j)
        opened_w = lax.dynamic_update_slice_in_dim(opened_w, got, (chip ^ j) * slab, 0)
    b_half = rows(b, core * half, half)
    d_sel = opened_w * select.astype(bf16)

    block = samples // n_group
    packed = party_swap(pack_rows(small, me ^ n_feat, block))
    other_small = [packed[k * block : (k + 1) * block].astype(f32) for k in range(6)]
    own_small = [rows(v, me * block, block).astype(f32) for v in small]

    e_own_a = opened(own_a, o_own_a)
    e_oth = opened(m_oth, o_oth)
    p_oth = dot(e_oth, d_sel) + dot(e_oth, b_half) + dot(a_oth, opened_w)
    e_own_b = opened(own_b, after(o_own_b, p_oth))
    p_sum = dot(a_mine, opened_w) + core_swap(p_oth)
    p_sum = p_sum + dot(e_own_a, d_sel[:quarter]) + dot(e_own_a, b_half[:quarter])
    p_sum = p_sum + dot(e_own_b, d_sel[quarter:]) + dot(e_own_b, b_half[quarter:])

    sums = {0: rows(p_sum, me * block, block)}
    for j in range(1, n_group):
        got = swap(rows(p_sum, (me ^ j) * block, block), group, n_group, j)
        q = j // n_feat
        sums[q] = sums[q] + got if q in sums else got

    def shifted(total, arrays):
        margin = total + arrays[0]
        return margin, margin - arrays[1]

    m_a, d_a = shifted(sums[0], own_small)
    m_b, d_b = shifted(sums[1], other_small)
    spread = d_a + d_b

    def masked_residual(margin, arrays, sel):
        _, l, q, k, lab, mask = arrays
        cubed = sel * (spread * spread * spread) + 3.0 * (spread * spread) * l
        cubed = cubed + 3.0 * spread * q + k
        res = 0.5 * sel + slope_one * margin - cube_coef * cubed - lab
        return narrow(res - mask, bf16)

    res = opened(masked_residual(m_a, own_small, select), masked_residual(m_b, other_small, 1.0 - select))

    res_own = jnp.zeros((samples, pheno), bf16)
    res_own = lax.dynamic_update_slice_in_dim(res_own, res, me * block, 0)
    for j in range(1, n_group):
        got = swap(res, group, n_group, j)
        res_own = lax.dynamic_update_slice_in_dim(res_own, got, (me ^ j) * block, 0)
    res_oth = core_swap(res_own)

    early_oth = dot_rows(e_oth, r_oth)
    early_a = dot_rows(e_own_a, r_own)
    early_b = dot_rows(e_own_b, r_own)
    base = lax.optimization_barrier(w - rate * gp.astype(f32))

    top = jnp.max(jnp.maximum(jnp.abs(res_own), jnp.abs(res_oth)), axis=0, keepdims=True).astype(f32)
    bound = 2 * samples * (5.0 * input_reach * top + 4.0 * input_reach * mask_reach)
    scale = jnp.exp2(jnp.ceil(jnp.log2(bound)) - 15.0)

    def chip_pairs(pairs):
        return [(2 * i + k, 2 * j + k) for i, j in pairs for k in (0, 1)]

    middle = n_chip // 2
    step = half // chunks
    zone = [chip_pairs([(d, d + 1), (n_chip - 1 - d, n_chip - 2 - d)]) for d in range(middle - 1)]
    centre = chip_pairs([(middle - 1, middle), (middle, middle - 1)])
    back = [chip_pairs([(d + 1, d), (n_chip - 2 - d, n_chip - 1 - d)]) for d in range(middle - 1)]

    def share_scale(v, pairs):
        return lax.ppermute(jnp.broadcast_to(v, (8, pheno)), "sample", pairs)[:1]

    rs_own = res_own * select.astype(bf16)
    rs_oth = res_oth * select.astype(bf16)
    vals = []
    token = res_oth
    for k in range(chunks):
        cols = slice(k * step, (k + 1) * step)
        e_part, early_part, off = (e_own_a, early_a, 0) if k < chunks // 2 else (e_own_b, early_b, quarter)
        own = slice(k * step - off, (k + 1) * step - off)
        g = early_oth[cols] + early_part[own] + dot_rows(e_part[:, own], after(rs_own, token))
        g = g + dot_rows(e_oth[:, cols], rs_oth)
        g = g + dot_rows(a_mine[:, cols], res_own)
        g = g + dot_rows(a_oth[:, cols], res_oth)
        v = g * (1.0 / scale)
        token = narrow(v, f16)
        vals.append((v, token))

    msgs = [m for _, m in vals]
    vals = [v for v, _ in vals]
    scales = scale
    inward = []
    for d in range(middle - 1):
        got_scale = share_scale(scales, zone[d])
        wider = 2.0 * jnp.maximum(scales, got_scale)
        inward.append((scales / wider, got_scale / wider))
        scales = wider
    mid_scale = share_scale(scales, centre)
    wider = 2.0 * jnp.maximum(scales, mid_scale)
    keep_mid, take_mid = scales / wider, mid_scale / wider
    final_scale = wider
    for d in reversed(range(middle - 1)):
        got_scale = share_scale(final_scale, back[d])
        outer = (chip == d) | (chip == n_chip - 1 - d)
        final_scale = jnp.where(outer, got_scale, final_scale)
    final_rate = rate * final_scale

    n_in = middle - 1
    stages = [("in", d) for d in range(n_in)] + [("mid", 0)] + [("out", d) for d in reversed(range(n_in))]
    result = base
    flight = {}
    for k in range(chunks):
        kind, d = stages[0]
        flight[k] = lax.ppermute(msgs[k], "sample", zone[d] if kind == "in" else centre)
    order = sorted((k + st, st, k) for k in range(chunks) for st in range(len(stages)))
    for _, st, k in order:
        kind, d = stages[st]
        got = after(flight[k], token)
        if kind == "in":
            keep, take = inward[d]
            vals[k] = vals[k] * keep + got.astype(f32) * take
            msgs[k] = narrow(vals[k], f16)
        elif kind == "mid":
            msgs[k] = narrow(msgs[k].astype(f32) * keep_mid + got.astype(f32) * take_mid, f16)
        else:
            outer = (chip == d) | (chip == n_chip - 1 - d)
            msgs[k] = jnp.where(outer, got, msgs[k])
        token = msgs[k]
        if st + 1 < len(stages):
            kind, d = stages[st + 1]
            pairs = zone[d] if kind == "in" else centre if kind == "mid" else back[d]
            flight[k] = lax.ppermute(msgs[k], "sample", pairs)
        else:
            theirs = core_swap(msgs[k])
            for value, who in ((msgs[k], core), (theirs, 1 - core)):
                where = who * half + k * step
                new = rows(result, where, step) - final_rate * value.astype(f32)
                result = lax.dynamic_update_slice_in_dim(result, new, where, 0)
    return result[None]


def solution(mesh):
    placed = (
        P("party", "sample", "feat"),
        P("party", "sample", "feat"),
        P("party", "feat", None),
        P("party", "feat", None),
        P("party", "sample", None),
        P("party", "sample", None),
        P("party", "sample", None),
        P("party", "sample", None),
        P("party", "sample", None),
        P("party", "sample", None),
        P("party", "feat", None),
    )
    return jax.shard_map(step_fn, mesh=mesh, in_specs=placed, out_specs=P("party", "feat", None), check_vma=False)
```

```python
import jax
import jax.numpy as jnp
from jax import lax
from jax.experimental import pallas as pl
from jax.experimental.pallas import tpu as pltpu
from jax.sharding import PartitionSpec as P


learn_rate = 64.0
slope_one = 0.197
cube_coef = 0.004
input_reach = 3.0
mask_reach = 3.0
chunks = 4

f32 = jnp.float32
bf16 = jnp.bfloat16
f16 = jnp.float16


def swap(value, axes, size, bit):
    return lax.ppermute(value, axes, [(i, i ^ bit) for i in range(size)])


def after(value, token):
    return lax.optimization_barrier((value, token))[0]


def narrow(value, dtype):
    info = jnp.finfo(dtype)
    return lax.reduce_precision(value, info.nexp, info.nmant).astype(dtype)


def opened(p, q):
    return narrow(p.astype(f32) + q.astype(f32), bf16)


def dot(left, right):
    return jnp.dot(left, right, preferred_element_type=f32)


def dot_rows(left, right):
    return lax.dot_general(left, right, (((0,), (0,)), ((), ())), preferred_element_type=f32)


def rows(array, first, number):
    return lax.dynamic_slice_in_dim(array, first, number, 0)


def pack_rows(arrays, block_index, block):
    width = arrays[0].shape[1]

    def body(index, *refs):
        for k, ref in enumerate(refs[:-1]):
            refs[-1][k * block : (k + 1) * block, :] = ref[...]

    spec = pl.BlockSpec((block, width), lambda i, index: (index[0], 0))
    number = len(arrays) * block
    return pl.pallas_call(
        body,
        out_shape=jax.ShapeDtypeStruct((number, width), arrays[0].dtype),
        grid_spec=pltpu.PrefetchScalarGridSpec(
            num_scalar_prefetch=1,
            grid=(1,),
            in_specs=[spec] * len(arrays),
            out_specs=pl.BlockSpec((number, width), lambda i, index: (0, 0)),
        ),
        cost_estimate=pl.CostEstimate(flops=0, bytes_accessed=4 * number * width, transcendentals=0),
        name="pack_rows",
    )(jnp.reshape(block_index, (1,)), *arrays)


def step_fn(x, a, w, b, c_sh, lin, sq, cube, y, r, gp):
    x, a, w, b, gp = x[0], a[0], w[0], b[0], gp[0]
    small = (c_sh[0], lin[0], sq[0], cube[0], y[0], r[0])
    n_sample, n_feat, n_party = (lax.axis_size(k) for k in ("sample", "feat", "party"))
    party, s, feat = (lax.axis_index(k) for k in ("party", "sample", "feat"))
    core = s % 2
    chip = s // 2
    n_chip = n_sample // 2
    group = ("party", "feat")
    n_group = n_party * n_feat
    me = party * n_feat + feat
    samples = x.shape[0]
    pheno = w.shape[1]
    half = x.shape[1] // 2
    quarter = half // 2
    first = core == 0
    select = (party == 0).astype(f32)
    total_samples = samples * n_sample
    rate = learn_rate / total_samples

    def core_swap(v):
        return swap(v, "sample", n_sample, 1)

    def party_swap(v):
        return swap(v, "party", n_party, 1)

    def pick(v):
        return jnp.where(first, v[:, :half], v[:, half:]), jnp.where(first, v[:, half:], v[:, :half])

    slab = half // n_chip
    at = core * half + chip * slab
    w_m = narrow(rows(w, at, slab) - rows(b, at, slab).astype(f32), bf16)
    w_o = party_swap(w_m)

    m = narrow(x.astype(f32) - a.astype(f32), bf16)
    m_mine, m_send = pick(m)
    a_mine, a_send = pick(a)
    m_oth = core_swap(m_send)
    own_a, own_b = m_mine[:, :quarter], m_mine[:, quarter:]
    o_own_a = party_swap(own_a)
    o_oth = party_swap(m_oth)
    o_own_b = party_swap(own_b)
    a_oth = core_swap(a_send)
    r_own = small[5]
    r_oth = core_swap(r_own)

    d_slab = opened(w_m, w_o)
    opened_w = jnp.zeros((half, pheno), bf16)
    opened_w = lax.dynamic_update_slice_in_dim(opened_w, d_slab, chip * slab, 0)
    for j in range(1, n_chip):
        got = swap(d_slab, "sample", n_sample, 2 * j)
        opened_w = lax.dynamic_update_slice_in_dim(opened_w, got, (chip ^ j) * slab, 0)
    b_half = rows(b, core * half, half)
    d_sel = opened_w * select.astype(bf16)

    block = samples // n_group
    base = w - rate * gp.astype(f32)
    packed = pack_rows(small, me ^ n_feat, block)
    packed, base = lax.optimization_barrier((packed, base))
    packed = party_swap(packed)
    other_small = [packed[k * block : (k + 1) * block].astype(f32) for k in range(6)]
    own_small = [rows(v, me * block, block).astype(f32) for v in small]

    e_own_a = opened(own_a, o_own_a)
    e_oth = opened(m_oth, o_oth)
    p_oth = dot(e_oth, d_sel) + dot(e_oth, b_half) + dot(a_oth, opened_w)
    p_own = dot(a_mine, opened_w) + dot(e_own_a, d_sel[:quarter]) + dot(e_own_a, b_half[:quarter])
    early_oth = dot_rows(e_oth, r_oth)
    early_a = dot_rows(e_own_a, r_own)
    e_own_b = opened(own_b, after(o_own_b, (p_oth, p_own, early_oth, early_a)))
    p_sum = p_own + core_swap(p_oth)
    p_sum = p_sum + dot(e_own_b, d_sel[quarter:]) + dot(e_own_b, b_half[quarter:])

    sums = {0: rows(p_sum, me * block, block)}
    for j in range(1, n_group):
        got = swap(rows(p_sum, (me ^ j) * block, block), group, n_group, j)
        q = j // n_feat
        sums[q] = sums[q] + got if q in sums else got

    def shifted(total, arrays):
        margin = total + arrays[0]
        return margin, margin - arrays[1]

    m_a, d_a = shifted(sums[0], own_small)
    m_b, d_b = shifted(sums[1], other_small)
    spread = d_a + d_b

    def masked_residual(margin, arrays, sel):
        _, l, q, k, lab, mask = arrays
        cubed = sel * (spread * spread * spread) + 3.0 * (spread * spread) * l
        cubed = cubed + 3.0 * spread * q + k
        res = 0.5 * sel + slope_one * margin - cube_coef * cubed - lab
        return narrow(res - mask, bf16)

    res = opened(masked_residual(m_a, own_small, select), masked_residual(m_b, other_small, 1.0 - select))

    res_own = jnp.zeros((samples, pheno), bf16)
    res_own = lax.dynamic_update_slice_in_dim(res_own, res, me * block, 0)
    for j in range(1, n_group):
        got = swap(res, group, n_group, j)
        res_own = lax.dynamic_update_slice_in_dim(res_own, got, (me ^ j) * block, 0)
    res_oth = core_swap(res_own)

    early_b = dot_rows(e_own_b, r_own)

    top = jnp.max(jnp.maximum(jnp.abs(res_own), jnp.abs(res_oth)), axis=0, keepdims=True).astype(f32)
    bound = 2 * samples * (5.0 * input_reach * top + 4.0 * input_reach * mask_reach)
    scale = jnp.exp2(jnp.ceil(jnp.log2(bound)) - 15.0)

    def chip_pairs(pairs):
        return [(2 * i + k, 2 * j + k) for i, j in pairs for k in (0, 1)]

    middle = n_chip // 2
    step = half // chunks
    zone = [chip_pairs([(d, d + 1), (n_chip - 1 - d, n_chip - 2 - d)]) for d in range(middle - 1)]
    centre = chip_pairs([(middle - 1, middle), (middle, middle - 1)])
    back = [chip_pairs([(d + 1, d), (n_chip - 2 - d, n_chip - 1 - d)]) for d in range(middle - 1)]

    def share_scale(v, pairs):
        return lax.ppermute(jnp.broadcast_to(v, (8, pheno)), "sample", pairs)[:1]

    rs_own = res_own * select.astype(bf16)
    rs_oth = res_oth * select.astype(bf16)
    vals = []
    token = res
    for k in range(chunks):
        cols = slice(k * step, (k + 1) * step)
        e_part, early_part, off = (e_own_a, early_a, 0) if k < chunks // 2 else (e_own_b, early_b, quarter)
        own = slice(k * step - off, (k + 1) * step - off)
        s_own, s_oth, f_own, f_oth = after((rs_own, rs_oth, res_own, res_oth), token)
        g = early_oth[cols] + early_part[own] + dot_rows(e_part[:, own], s_own)
        g = g + dot_rows(a_mine[:, cols], f_own)
        g = g + dot_rows(e_oth[:, cols], s_oth)
        g = g + dot_rows(a_oth[:, cols], f_oth)
        v = g * (1.0 / scale)
        token = narrow(v, f16)
        vals.append((v, token))

    msgs = [m for _, m in vals]
    vals = [v for v, _ in vals]
    scales = scale
    inward = []
    for d in range(middle - 1):
        got_scale = share_scale(scales, zone[d])
        wider = 2.0 * jnp.maximum(scales, got_scale)
        inward.append((scales / wider, got_scale / wider))
        scales = wider
    mid_scale = share_scale(scales, centre)
    wider = 2.0 * jnp.maximum(scales, mid_scale)
    keep_mid, take_mid = scales / wider, mid_scale / wider
    final_scale = wider
    for d in reversed(range(middle - 1)):
        got_scale = share_scale(final_scale, back[d])
        outer = (chip == d) | (chip == n_chip - 1 - d)
        final_scale = jnp.where(outer, got_scale, final_scale)
    final_rate = rate * final_scale

    n_in = middle - 1
    stages = [("in", d) for d in range(n_in)] + [("mid", 0)] + [("out", d) for d in reversed(range(n_in))]
    theirs = []
    flight = {}
    for k in range(chunks):
        kind, d = stages[0]
        flight[k] = lax.ppermute(msgs[k], "sample", zone[d] if kind == "in" else centre)
    order = sorted((k + st, st, k) for k in range(chunks) for st in range(len(stages)))
    for _, st, k in order:
        kind, d = stages[st]
        got = after(flight[k], token)
        if kind == "in":
            keep, take = inward[d]
            vals[k] = vals[k] * keep + got.astype(f32) * take
            msgs[k] = narrow(vals[k], f16)
        elif kind == "mid":
            msgs[k] = narrow(msgs[k].astype(f32) * keep_mid + got.astype(f32) * take_mid, f16)
        else:
            outer = (chip == d) | (chip == n_chip - 1 - d)
            msgs[k] = jnp.where(outer, got, msgs[k])
        token = msgs[k]
        if st + 1 < len(stages):
            kind, d = stages[st + 1]
            pairs = zone[d] if kind == "in" else centre if kind == "mid" else back[d]
            flight[k] = lax.ppermute(msgs[k], "sample", pairs)
        else:
            theirs.append(core_swap(msgs[k]))
    mine = jnp.concatenate([msgs[k] for k in range(chunks)], 0)
    theirs = jnp.concatenate(theirs, 0)
    low = jnp.where(first, mine, theirs).astype(f32)
    high = jnp.where(first, theirs, mine).astype(f32)
    result = base - final_rate * jnp.concatenate([low, high], 0)
    return result[None]


def solution(mesh):
    placed = (
        P("party", "sample", "feat"),
        P("party", "sample", "feat"),
        P("party", "feat", None),
        P("party", "feat", None),
        P("party", "sample", None),
        P("party", "sample", None),
        P("party", "sample", None),
        P("party", "sample", None),
        P("party", "sample", None),
        P("party", "sample", None),
        P("party", "feat", None),
    )
    return jax.shard_map(step_fn, mesh=mesh, in_specs=placed, out_specs=P("party", "feat", None), check_vma=False)
```

```python
import jax
import jax.numpy as jnp
from jax import lax
from jax.experimental import pallas as pl
from jax.experimental.pallas import tpu as pltpu
from jax.sharding import PartitionSpec as P


learn_rate = 64.0
slope_one = 0.197
cube_coef = 0.004
input_reach = 3.0
mask_reach = 3.0
chunks = 4

f32 = jnp.float32
bf16 = jnp.bfloat16
f16 = jnp.float16


def swap(value, axes, size, bit):
    return lax.ppermute(value, axes, [(i, i ^ bit) for i in range(size)])


def after(value, token):
    return lax.optimization_barrier((value, token))[0]


def narrow(value, dtype):
    info = jnp.finfo(dtype)
    return lax.reduce_precision(value, info.nexp, info.nmant).astype(dtype)


def opened(p, q):
    return narrow(p.astype(f32) + q.astype(f32), bf16)


def dot(left, right):
    return jnp.dot(left, right, preferred_element_type=f32)


def dot_rows(left, right):
    return lax.dot_general(left, right, (((0,), (0,)), ((), ())), preferred_element_type=f32)


def rows(array, first, number):
    return lax.dynamic_slice_in_dim(array, first, number, 0)


def pack_rows(arrays, block_index, block):
    width = arrays[0].shape[1]

    def body(index, *refs):
        for k, ref in enumerate(refs[:-1]):
            refs[-1][k * block : (k + 1) * block, :] = ref[...]

    spec = pl.BlockSpec((block, width), lambda i, index: (index[0], 0))
    number = len(arrays) * block
    return pl.pallas_call(
        body,
        out_shape=jax.ShapeDtypeStruct((number, width), arrays[0].dtype),
        grid_spec=pltpu.PrefetchScalarGridSpec(
            num_scalar_prefetch=1,
            grid=(1,),
            in_specs=[spec] * len(arrays),
            out_specs=pl.BlockSpec((number, width), lambda i, index: (0, 0)),
        ),
        cost_estimate=pl.CostEstimate(flops=0, bytes_accessed=4 * number * width, transcendentals=0),
        name="pack_rows",
    )(jnp.reshape(block_index, (1,)), *arrays)


def mask_slot(x, a, block_index, width):
    samples = x.shape[0]
    tall = samples // 2

    def body(index, x_ref, a_ref, m_ref, a_out):
        own = a_ref[...]
        m_ref[...] = (x_ref[...].astype(f32) - own.astype(f32)).astype(bf16)
        a_out[...] = own

    spec = pl.BlockSpec((tall, width), lambda i, index: (i, index[0]))
    out = pl.BlockSpec((tall, width), lambda i, index: (i, 0))
    shape = jax.ShapeDtypeStruct((samples, width), bf16)
    return pl.pallas_call(
        body,
        out_shape=(shape, shape),
        grid_spec=pltpu.PrefetchScalarGridSpec(
            num_scalar_prefetch=1, grid=(2,), in_specs=[spec, spec], out_specs=(out, out)
        ),
        cost_estimate=pl.CostEstimate(
            flops=samples * width, bytes_accessed=8 * samples * width, transcendentals=0
        ),
        name="mask_slot",
    )(jnp.reshape(block_index, (1,)), x, a)


def wave(n_hop):
    grad_at, in_at = (0, 4, 16, 19.5), (7, 14, 27, 33)
    steps = [(grad_at[k] if st == 0 else in_at[k] + 8.5 * (st - 1), st, k) for k in range(chunks) for st in range(n_hop + 1)]
    return [(st, k) for _, st, k in sorted(steps)]


def step_fn(x, a, w, b, c_sh, lin, sq, cube, y, r, gp):
    x, a, w, b, gp = x[0], a[0], w[0], b[0], gp[0]
    small = (c_sh[0], lin[0], sq[0], cube[0], y[0], r[0])
    n_sample, n_feat, n_party = (lax.axis_size(k) for k in ("sample", "feat", "party"))
    party, s, feat = (lax.axis_index(k) for k in ("party", "sample", "feat"))
    core = s % 2
    chip = s // 2
    n_chip = n_sample // 2
    group = ("party", "feat")
    n_group = n_party * n_feat
    me = party * n_feat + feat
    samples = x.shape[0]
    pheno = w.shape[1]
    half = x.shape[1] // 2
    quarter = half // 2
    first = core == 0
    select = (party == 0).astype(f32)
    total_samples = samples * n_sample
    rate = learn_rate / total_samples

    def core_swap(v):
        return swap(v, "sample", n_sample, 1)

    def party_swap(v):
        return swap(v, "party", n_party, 1)

    slab = half // n_chip
    at = core * half + chip * slab
    w_m = narrow(rows(w, at, slab) - rows(b, at, slab).astype(f32), bf16)
    w_o = party_swap(w_m)

    def slot(core_index, quarter_index):
        return mask_slot(x, a, 2 * core_index + quarter_index, quarter)

    other_party, other_core = 1 - party, 1 - core
    m_send, a_send = slot(other_core, other_party)
    m_oth_rest = core_swap(m_send)
    m_own_rest, a_own_rest = slot(core, other_party)
    o_oth_crit = party_swap(m_oth_rest)
    b_send = rows(b, core * half + other_party * quarter, quarter)
    b_other = party_swap(b_send)
    o_own_crit = party_swap(m_own_rest)

    d_slab = opened(w_m, w_o)
    opened_w = jnp.zeros((half, pheno), bf16)
    opened_w = lax.dynamic_update_slice_in_dim(opened_w, d_slab, chip * slab, 0)
    for j in range(1, n_chip):
        got = swap(d_slab, "sample", n_sample, 2 * j)
        opened_w = lax.dynamic_update_slice_in_dim(opened_w, got, (chip ^ j) * slab, 0)

    a_oth_rest = core_swap(a_send)
    m_send, a_send = slot(other_core, party)
    m_oth_crit = core_swap(m_send)
    a_oth_crit = core_swap(a_send)
    m_own_crit, a_own_crit = slot(core, party)
    r_own = small[5]
    r_oth = core_swap(r_own)

    block = samples // n_group
    base = w - rate * gp.astype(f32)
    packed = pack_rows(small, me ^ n_feat, block)
    own_rows = pack_rows(small, me, block)
    packed, base = lax.optimization_barrier((packed, base))
    packed = party_swap(packed)

    def constants(packed_rows, sel):
        c_, l_, q_, k_, y_, r_ = (packed_rows[i * block : (i + 1) * block].astype(f32) for i in range(6))
        return c_, c_ - l_, 3.0 * l_, 3.0 * q_, 0.5 * sel - cube_coef * k_ - y_ - r_

    own_const = lax.optimization_barrier(constants(own_rows, select))

    d_crit = rows(opened_w, party * quarter, quarter)
    d_rest = rows(opened_w, other_party * quarter, quarter)
    b_both = jnp.concatenate([rows(b, core * half + party * quarter, quarter), b_other], 1)
    d_both = jnp.concatenate([d_crit * select.astype(bf16), d_crit * (1.0 - select).astype(bf16)], 1)
    b_both, d_both = lax.optimization_barrier((b_both, d_both))

    def share_part(crit, rest):
        part = dot(crit, d_crit) + dot(rest, d_rest)
        return jnp.pad(part, ((0, 0), (0, pheno)))

    def open_part(e):
        return dot(e, d_both) + dot(e, b_both)

    e_oth_crit = opened(m_oth_crit, o_oth_crit)
    part_oth = share_part(a_oth_crit, a_oth_rest) + open_part(e_oth_crit)
    part_own = share_part(a_own_crit, a_own_rest)
    early_oth = dot_rows(e_oth_crit, r_oth)
    e_own_crit = opened(m_own_crit, after(o_own_crit, (part_oth, part_own, early_oth)))
    part = part_own + core_swap(part_oth) + open_part(e_own_crit)

    own_part = rows(part, me * block, block)
    sums = [own_part[:, :pheno], own_part[:, pheno:]]
    for j in range(1, n_group):
        got = swap(rows(part, (me ^ j) * block, block), group, n_group, j)
        pair = got[:, :pheno], got[:, pheno:]
        own_first = j < n_feat
        sums = [sums[0] + pair[0 if own_first else 1], sums[1] + pair[1 if own_first else 0]]
        if j == 1:
            packed = after(packed, got)
    other_const = lax.optimization_barrier(constants(packed, 1.0 - select))

    spread = (sums[0] + own_const[1]) + (sums[1] + other_const[1])

    def masked_residual(total, arrays, sel):
        c_, _, l_, q_, rest = arrays
        cubed = sel * (spread * spread * spread) + (spread * spread) * l_ + spread * q_
        return narrow(rest + slope_one * (total + c_) - cube_coef * cubed, bf16)

    res = opened(
        masked_residual(sums[0], own_const, select), masked_residual(sums[1], other_const, 1.0 - select)
    )

    res_own = jnp.zeros((samples, pheno), bf16)
    res_own = lax.dynamic_update_slice_in_dim(res_own, res, me * block, 0)
    for j in range(1, n_group):
        got = swap(res, group, n_group, j)
        res_own = lax.dynamic_update_slice_in_dim(res_own, got, (me ^ j) * block, 0)
    res_oth = core_swap(res_own)

    early_crit = early_oth + dot_rows(e_own_crit, r_own)
    o_oth_rest = party_swap(m_oth_crit)
    o_own_rest = party_swap(m_own_crit)

    top = jnp.max(jnp.maximum(jnp.abs(res_own), jnp.abs(res_oth)), axis=0, keepdims=True).astype(f32)
    bound = 2 * samples * (5.0 * input_reach * top + 4.0 * input_reach * mask_reach)
    power = jnp.ceil(jnp.log2(bound)) - 15.0
    shrink = jnp.exp2(-power)

    def chip_pairs(pairs):
        return [(2 * i + k, 2 * j + k) for i, j in pairs for k in (0, 1)]

    middle = n_chip // 2
    n_in = middle - 1
    lead = max(128, quarter * 3 // 8 // 128 * 128)
    sizes = (lead, quarter - lead, quarter - lead, lead)
    starts = (0, lead, quarter, half - lead)
    zone = [chip_pairs([(d, d + 1), (n_chip - 1 - d, n_chip - 2 - d)]) for d in range(n_in)]
    centre = chip_pairs([(middle - 1, middle), (middle, middle - 1)])
    back = [chip_pairs([(d + 1, d), (n_chip - 2 - d, n_chip - 1 - d)]) for d in range(n_in)]

    hops = zone + [centre] + back[::-1]
    rs_own = res_own * select.astype(bf16)
    rs_oth = res_oth * select.astype(bf16)
    step = sizes[0]
    is_chunk_row = lax.broadcasted_iota(jnp.int32, (step + 16, pheno), 0) < step

    def with_power(value, exponent):
        padded = lax.pad(value, jnp.zeros((), f16), ((0, 16, 0), (0, 0, 0)))
        return jnp.where(is_chunk_row, padded, exponent.astype(f16))

    vals, msgs, flight, factors = {}, {}, {}, {}
    token = res
    final_rate = None

    rest = {}

    def gradient(k):
        cols = slice(starts[k] % quarter, starts[k] % quarter + sizes[k])
        s_own, s_oth, f_own, f_oth = after((rs_own, rs_oth, res_own, res_oth), token)
        if k < chunks // 2:
            e_own, e_oth, a_own, a_oth = e_own_crit, e_oth_crit, a_own_crit, a_oth_crit
            g = early_crit[cols]
        else:
            if not rest:
                rest[0] = opened(m_own_rest, after(o_own_rest, token))
                rest[1] = opened(m_oth_rest, after(o_oth_rest, token))
            e_own, e_oth, a_own, a_oth = rest[0], rest[1], a_own_rest, a_oth_rest
            g = dot_rows(e_own[:, cols], r_own) + dot_rows(e_oth[:, cols], r_oth)
        g = g + dot_rows(e_own[:, cols], s_own) + dot_rows(a_own[:, cols], f_own)
        g = g + dot_rows(e_oth[:, cols], s_oth) + dot_rows(a_oth[:, cols], f_oth)
        return g * shrink

    last = len(hops)
    for st, k in wave(last):
        if st == 0:
            vals[k] = gradient(k)
            msgs[k] = narrow(vals[k], f16)
        elif st <= last:
            got = after(flight[k], token)
            if k == 0:
                got_power = got[step : step + 1].astype(f32)
                got = got[:step]
            if st <= n_in + 1:
                if k == 0:
                    power_out = jnp.maximum(power, got_power) + 1.0
                    factors[st] = jnp.exp2(power - power_out), jnp.exp2(got_power - power_out)
                    power = power_out
                keep, take = factors[st]
                if st <= n_in:
                    vals[k] = vals[k] * keep + got.astype(f32) * take
                    msgs[k] = narrow(vals[k], f16)
                else:
                    msgs[k] = narrow(msgs[k].astype(f32) * keep + got.astype(f32) * take, f16)
            else:
                d = n_in - 1 - (st - n_in - 2)
                outer = (chip == d) | (chip == n_chip - 1 - d)
                msgs[k] = jnp.where(outer, got, msgs[k])
                if k == 0:
                    power_out = jnp.where(outer, got_power, power)
                    power = power_out
            if st == last and k == 0:
                final_rate = rate * jnp.exp2(power)
        else:
            continue
        token = msgs[k]
        if st < last:
            message = with_power(msgs[k], power) if k == 0 else msgs[k]
            flight[k] = lax.ppermute(message, "sample", hops[st])
        else:
            flight[k] = core_swap(msgs[k])

    def quarters(parts):
        crit = jnp.concatenate(parts[: chunks // 2], 0)
        others = jnp.concatenate(parts[chunks // 2 :], 0)
        return jnp.where(party == 0, crit, others), jnp.where(party == 0, others, crit)

    mine = quarters([msgs[k] for k in range(chunks)])
    theirs = quarters([flight[k] for k in range(chunks)])
    low = [jnp.where(first, p, q) for p, q in zip(mine, theirs)]
    high = [jnp.where(first, q, p) for p, q in zip(mine, theirs)]
    result = base - final_rate * jnp.concatenate(low + high, 0).astype(f32)
    return result[None]


def solution(mesh):
    placed = (
        P("party", "sample", "feat"),
        P("party", "sample", "feat"),
        P("party", "feat", None),
        P("party", "feat", None),
        P("party", "sample", None),
        P("party", "sample", None),
        P("party", "sample", None),
        P("party", "sample", None),
        P("party", "sample", None),
        P("party", "sample", None),
        P("party", "feat", None),
    )
    return jax.shard_map(
        step_fn, mesh=mesh, in_specs=placed, out_specs=P("party", "feat", None), check_vma=False
    )
```
